32 devices in a mesh: lon: 8 (over z, x), lat: 4 (over y, core).
Axes of the slice: x: 2, y: 2, z: 4, core: 2. Of those that a mesh axis runs over, the one named last changes fastest.
Arguments:
- inputs: bfloat16 [256, 32, 2048], P(None, 'lat', 'lon'), may hold values from -6 to 6
- cotangent: bfloat16 [256, 32, 2048], P(None, 'lat', 'lon'), may hold values from -6 to 6
- mixing: bfloat16 [9, 256, 256], replicated, may hold values from -0.125 to 0.125
- filters: bfloat16 [9, 32, 3, 33], P(None, 'lat'), may hold values from -0.8984375 to 0.8984375
- support: int32 [32], P('lat'), may hold values from 1 to 16, as said below
Outputs:
- input_grad: bfloat16 [256, 32, 2048], P(None, 'lat', 'lon')
- weight_grad: float32 [9, 256, 256], replicated
The draws below stay inside these ranges and needn't reach their ends.
Inputs may be any that keep to these rules, and one draw needn't show every extreme that they name: support[i] is the widest longitude offset, in cells, reached by the filter of latitude row i.
All inputs are finite; a program needn't handle non-finite values.
Results may differ from the reference program's by a relative error of at most 0.0051.
Values may be sent and summed in bfloat16 or wider, within the bound.
A program may use at most 192 MiB of HBM per device.

```python
import math
import jax
import jax.numpy as jnp
from jax import lax

CHANNELS = 256
KERNELS = 9
LAT_REACH = 1
LON_REACH = 16
NLAT = 32
NLON = 2048


def draw_support(key, part):
    first_key, second_key, third_key = jax.random.split(key, 3)
    rows = jnp.arange(NLAT, dtype=jnp.int32)
    distance = jnp.abs(2 * rows + 1 - NLAT)
    base_width = 1 + (LON_REACH - 4) * distance * distance // (NLAT * NLAT)
    jitter = jax.random.randint(first_key, (NLAT,), 0, 4, dtype=jnp.int32)
    widths = jnp.minimum(base_width + jitter, LON_REACH)
    widest = jax.random.randint(second_key, (), 0, NLAT, dtype=jnp.int32)
    narrow = (widest + 1 + jax.random.randint(third_key, (), 0, NLAT - 1, dtype=jnp.int32)) % NLAT
    widths = widths.at[widest].set(LON_REACH)
    widths = widths.at[narrow].set(1)
    return widths.astype(jnp.int32)


def shard_levels(own_key, shape, pieces, smallest, largest):
    gain, own = 1.0, jax.random.fold_in(own_key, 6)
    for dim, shards_of in pieces:
        heights = jnp.exp(jax.random.uniform(jax.random.fold_in(own, dim), (shards_of,), jnp.float32, smallest / len(pieces), largest / len(pieces)))
        gain = gain * jnp.repeat(heights, shape[dim] // shards_of).reshape([-1 if axis == dim else 1 for axis in range(len(shape))])
    return gain


def noise(rng, extent, deviation, limit, shards=(), kind=jnp.bfloat16):
    factor_of = shard_levels(rng, extent, shards, -0.22, 0.18) if shards else 1.0
    array = jax.random.normal(rng, extent, jnp.float32) * deviation * factor_of
    return jnp.minimum(jnp.maximum(array, -limit), limit).astype(kind)


def setup_inputs(seed: int = 0) -> dict:
    key_of = jax.random.split(jax.random.key(seed), 6)
    inputs = noise(key_of[0], (CHANNELS, NLAT, NLON), 1.0, 6.0, ((1, 4), (2, 8)))
    cotangent = noise(key_of[1], (CHANNELS, NLAT, NLON), 1.0, 6.0, ((1, 4), (2, 8)))
    mixing = noise(key_of[2], (KERNELS, CHANNELS, CHANNELS), (KERNELS * CHANNELS) ** -0.5, 0.125)
    filters = noise(key_of[3], (KERNELS, NLAT, 2 * LAT_REACH + 1, 2 * LON_REACH + 1), 0.15, 0.8984375, ((1, 4),))
    support = draw_support(jax.random.fold_in(key_of[5], 71), 0)
    return {"inputs": inputs, "cotangent": cotangent, "mixing": mixing, "filters": filters, "support": support}


def masked_filters(filters, support):
    offsets = jnp.arange(2 * LON_REACH + 1, dtype=jnp.int32) - LON_REACH
    keep = (jnp.abs(offsets)[None, :] <= support[:, None]).astype(jnp.bfloat16)
    return filters * keep[None, :, None, :]

def wrap_pad(field, row_axis):
    widths = [(0, 0)] * field.ndim
    widths[row_axis] = (LAT_REACH, LAT_REACH)
    padded = jnp.pad(field, widths)
    return jnp.concatenate([padded[..., NLON - LON_REACH:], padded, padded[..., :LON_REACH]], axis=-1)

def reference(inputs, cotangent, mixing, filters, support):
    coefs = masked_filters(filters, support)
    cot_pad = wrap_pad(cotangent, 1)
    coef_pad = jnp.pad(coefs, ((0, 0), (LAT_REACH, LAT_REACH), (0, 0), (0, 0)))
    mix_wide = mixing.astype(jnp.float32)
    tap_count = 2 * LON_REACH + 1
    band_rows = 2 * LAT_REACH + 1

    def row_step(grad_acc, row_index):
        total = jnp.zeros((KERNELS, CHANNELS, NLON), jnp.float32)
        for offset in range(band_rows):
            source = row_index - offset + 2 * LAT_REACH
            cot_row = lax.dynamic_index_in_dim(cot_pad, source, 1, False).astype(jnp.float32)
            row_coefs = lax.dynamic_index_in_dim(coef_pad, source, 1, False)[:, offset, :].astype(jnp.float32)
            windows = jnp.stack([cot_row[:, 2 * LON_REACH - shift_col:2 * LON_REACH - shift_col + NLON] for shift_col in range(tap_count)], -1)
            total = total + jnp.einsum('cwb,kb->kcw', windows, row_coefs)
        spread = total.astype(jnp.bfloat16)
        spread = lax.optimization_barrier(spread).astype(jnp.float32)
        input_row = lax.dynamic_index_in_dim(inputs, row_index, 1, False).astype(jnp.float32)
        grad_acc = grad_acc + jnp.einsum('kow,cw->koc', spread, input_row)
        grad_row = jnp.einsum('koc,kow->cw', mix_wide, spread).astype(jnp.bfloat16)
        return (grad_acc, grad_row)
    weight_grad, rows = lax.scan(row_step, jnp.zeros((KERNELS, CHANNELS, CHANNELS), jnp.float32), jnp.arange(NLAT, dtype=jnp.int32))
    weight_grad = weight_grad * (1.0 / math.sqrt(NLAT * NLON))
    input_grad = jnp.transpose(rows, (1, 0, 2))
    return (input_grad, weight_grad)
```

```python
import math

import jax
import jax.numpy as jnp
from jax import lax
from jax.sharding import PartitionSpec as P

LAT_REACH = 1
LON_REACH = 16


def with_halo(cells, sides, width, closed):
    for axis, dim in sides:
        count = lax.axis_size(axis)
        ends = count if closed else count - 1
        head = lax.slice_in_dim(cells, 0, width, axis=dim)
        tail = lax.slice_in_dim(cells, cells.shape[dim] - width, cells.shape[dim], axis=dim)
        cells = jnp.concatenate(
            [
                lax.ppermute(tail, axis, [(i, (i + 1) % count) for i in range(ends)]),
                cells,
                lax.ppermute(head, axis, [((i + 1) % count, i) for i in range(ends)]),
            ],
            axis=dim,
        )
    return cells


def halving_psum(x):
    stages = []
    for axis in ("lat", "lon"):
        bit = 1
        while bit < lax.axis_size(axis):
            stages.append((axis, bit))
            bit *= 2
    cur = x.reshape(-1, x.shape[-1])
    if cur.shape[0] % (2 ** len(stages)):
        return lax.psum(x, ("lon", "lat"))
    for axis, bit in stages:
        count = lax.axis_size(axis)
        side = (lax.axis_index(axis) // bit) % 2
        half = cur.shape[0] // 2
        keep = lax.dynamic_slice_in_dim(cur, side * half, half, 0)
        send = lax.dynamic_slice_in_dim(cur, (1 - side) * half, half, 0)
        cur = keep + lax.ppermute(send, axis, [(i, i ^ bit) for i in range(count)])
    for axis, bit in reversed(stages):
        count = lax.axis_size(axis)
        side = (lax.axis_index(axis) // bit) % 2
        other = lax.ppermute(cur, axis, [(i, i ^ bit) for i in range(count)])
        half = cur.shape[0]
        buf = jnp.zeros((2 * half, cur.shape[1]), cur.dtype)
        buf = lax.dynamic_update_slice_in_dim(buf, cur, side * half, 0)
        cur = lax.dynamic_update_slice_in_dim(buf, other, (1 - side) * half, 0)
    return cur.reshape(x.shape)


def spread_block(source, coef_source, row_first, rows, col_first, cols):
    kernels = coef_source.shape[0]
    chans = source.shape[0]
    span = LON_REACH
    reach = LAT_REACH
    tap_count = 2 * span + 1
    window = cols + 2 * span
    tap_axis = jnp.arange(tap_count, dtype=jnp.int32)[:, None, None]
    wide_axis = jnp.arange(window, dtype=jnp.int32)[None, :, None]
    cell_axis = jnp.arange(cols, dtype=jnp.int32)[None, None, :]
    selector = (cell_axis + 2 * span - wide_axis == tap_axis).astype(jnp.bfloat16)
    total = jnp.zeros((kernels, chans, rows, cols), jnp.float32)
    for offset in range(2 * reach + 1):
        start = row_first + 2 * reach - offset
        rows_in = source[:, start : start + rows, col_first : col_first + window]
        part_coefs = coef_source[:, start : start + rows, offset, :]
        tiles = jnp.einsum(
            "bpq,kib->kipq", selector, part_coefs, preferred_element_type=jnp.float32
        ).astype(jnp.bfloat16)
        total = total + jnp.einsum(
            "oip,kipq->koiq", rows_in, tiles, preferred_element_type=jnp.float32
        )
    return total.astype(jnp.bfloat16)


def local(inputs, cotangent, mixing, filters, support):
    chans, lat_rows, lon_cols = inputs.shape
    span = LON_REACH
    reach = LAT_REACH
    tap_count = 2 * span + 1
    offsets = jnp.arange(tap_count, dtype=jnp.int32) - span
    keep = (jnp.abs(offsets)[None, :] <= support[:, None]).astype(jnp.bfloat16)
    coefs = filters * keep[None, :, None, :]
    widened = with_halo(cotangent, (("lon", 2),), span, True)
    padded = with_halo(widened, (("lat", 1),), reach, False)
    coef_pad = with_halo(coefs, (("lat", 1),), reach, False)
    spread = spread_block(padded, coef_pad, 0, lat_rows, 0, lon_cols)
    local_grad = jnp.einsum("koiq,ciq->koc", spread, inputs, preferred_element_type=jnp.float32)
    total_cells = lat_rows * lax.axis_size("lat") * lon_cols * lax.axis_size("lon")
    weight_grad = halving_psum(local_grad) * (1.0 / math.sqrt(total_cells))
    input_grad = jnp.einsum(
        "koc,koiq->ciq", mixing, spread, preferred_element_type=jnp.float32
    ).astype(jnp.bfloat16)
    return (input_grad, weight_grad)


def solution(mesh):
    return jax.shard_map(
        local,
        mesh=mesh,
        in_specs=(
            P(None, "lat", "lon"),
            P(None, "lat", "lon"),
            P(),
            P(None, "lat", None, None),
            P("lat"),
        ),
        out_specs=(P(None, "lat", "lon"), P()),
        check_vma=False,
    )
```

```python
import math

import jax
import jax.numpy as jnp
from jax import lax
from jax.sharding import PartitionSpec as P

LAT_REACH = 1
LON_REACH = 16


def with_halo(cells, sides, width, closed):
    for axis, dim in sides:
        count = lax.axis_size(axis)
        ends = count if closed else count - 1
        head = lax.slice_in_dim(cells, 0, width, axis=dim)
        tail = lax.slice_in_dim(cells, cells.shape[dim] - width, cells.shape[dim], axis=dim)
        cells = jnp.concatenate(
            [
                lax.ppermute(tail, axis, [(i, (i + 1) % count) for i in range(ends)]),
                cells,
                lax.ppermute(head, axis, [((i + 1) % count, i) for i in range(ends)]),
            ],
            axis=dim,
        )
    return cells


def halving_psum(x):
    stages = []
    for axis in ("lat", "lon"):
        bit = 1
        while bit < lax.axis_size(axis):
            stages.append((axis, bit))
            bit *= 2
    cur = x.reshape(-1, x.shape[-1])
    if cur.shape[0] % (2 ** len(stages)):
        return lax.psum(x, ("lon", "lat"))
    for axis, bit in stages:
        count = lax.axis_size(axis)
        side = (lax.axis_index(axis) // bit) % 2
        half = cur.shape[0] // 2
        keep = lax.dynamic_slice_in_dim(cur, side * half, half, 0)
        send = lax.dynamic_slice_in_dim(cur, (1 - side) * half, half, 0)
        cur = keep + lax.ppermute(send, axis, [(i, i ^ bit) for i in range(count)])
    for axis, bit in reversed(stages):
        count = lax.axis_size(axis)
        side = (lax.axis_index(axis) // bit) % 2
        other = lax.ppermute(cur, axis, [(i, i ^ bit) for i in range(count)])
        half = cur.shape[0]
        buf = jnp.zeros((2 * half, cur.shape[1]), cur.dtype)
        buf = lax.dynamic_update_slice_in_dim(buf, cur, side * half, 0)
        cur = lax.dynamic_update_slice_in_dim(buf, other, (1 - side) * half, 0)
    return cur.reshape(x.shape)


def spread_block(source, coef_source, row_first, rows, col_first, cols):
    kernels = coef_source.shape[0]
    chans = source.shape[0]
    span = LON_REACH
    reach = LAT_REACH
    tap_count = 2 * span + 1
    window = cols + 2 * span
    tap_axis = jnp.arange(tap_count, dtype=jnp.int32)[:, None, None]
    wide_axis = jnp.arange(window, dtype=jnp.int32)[None, :, None]
    cell_axis = jnp.arange(cols, dtype=jnp.int32)[None, None, :]
    selector = (cell_axis + 2 * span - wide_axis == tap_axis).astype(jnp.bfloat16)
    total = jnp.zeros((kernels, chans, rows, cols), jnp.float32)
    for offset in range(2 * reach + 1):
        start = row_first + 2 * reach - offset
        rows_in = source[:, start : start + rows, col_first : col_first + window]
        part_coefs = coef_source[:, start : start + rows, offset, :]
        tiles = jnp.einsum(
            "bpq,kib->kipq", selector, part_coefs, preferred_element_type=jnp.float32
        ).astype(jnp.bfloat16)
        total = total + jnp.einsum(
            "oip,kipq->koiq", rows_in, tiles, preferred_element_type=jnp.float32
        )
    return total.astype(jnp.bfloat16)


def local(inputs, cotangent, mixing, filters, support):
    chans, lat_rows, lon_cols = inputs.shape
    span = LON_REACH
    reach = LAT_REACH
    tap_count = 2 * span + 1
    offsets = jnp.arange(tap_count, dtype=jnp.int32) - span
    keep = (jnp.abs(offsets)[None, :] <= support[:, None]).astype(jnp.bfloat16)
    coefs = filters * keep[None, :, None, :]
    widened = with_halo(cotangent, (("lon", 2),), span, True)
    padded = with_halo(widened, (("lat", 1),), reach, False)
    coef_pad = with_halo(coefs, (("lat", 1),), reach, False)
    total_cells = lat_rows * lax.axis_size("lat") * lon_cols * lax.axis_size("lon")
    kernels = coefs.shape[0]
    groups = 3 if kernels % 3 == 0 else 1
    size = kernels // groups
    grad_parts = []
    input_acc = None
    for g in range(groups):
        part = slice(g * size, (g + 1) * size)
        spread = spread_block(padded, coef_pad[part], 0, lat_rows, 0, lon_cols)
        local_grad = jnp.einsum("koiq,ciq->koc", spread, inputs, preferred_element_type=jnp.float32)
        grad_parts.append(halving_psum(local_grad))
        term = jnp.einsum(
            "koc,koiq->ciq", mixing[part], spread, preferred_element_type=jnp.float32
        )
        input_acc = term if input_acc is None else input_acc + term
    weight_grad = jnp.concatenate(grad_parts, axis=0) * (1.0 / math.sqrt(total_cells))
    input_grad = input_acc.astype(jnp.bfloat16)
    return (input_grad, weight_grad)


def solution(mesh):
    return jax.shard_map(
        local,
        mesh=mesh,
        in_specs=(
            P(None, "lat", "lon"),
            P(None, "lat", "lon"),
            P(),
            P(None, "lat", None, None),
            P("lat"),
        ),
        out_specs=(P(None, "lat", "lon"), P()),
        check_vma=False,
    )
```

```python
import math

import jax
import jax.numpy as jnp
from jax import lax
from jax.sharding import PartitionSpec as P

LAT_REACH = 1
LON_REACH = 16


def with_halo(cells, sides, width, closed):
    for axis, dim in sides:
        count = lax.axis_size(axis)
        ends = count if closed else count - 1
        head = lax.slice_in_dim(cells, 0, width, axis=dim)
        tail = lax.slice_in_dim(cells, cells.shape[dim] - width, cells.shape[dim], axis=dim)
        cells = jnp.concatenate(
            [
                lax.ppermute(tail, axis, [(i, (i + 1) % count) for i in range(ends)]),
                cells,
                lax.ppermute(head, axis, [((i + 1) % count, i) for i in range(ends)]),
            ],
            axis=dim,
        )
    return cells


def halving_psum(x):
    stages = []
    for axis in ("lat", "lon"):
        bit = 1
        while bit < lax.axis_size(axis):
            stages.append((axis, bit))
            bit *= 2
    cur = x.reshape(-1, x.shape[-1])
    if cur.shape[0] % (2 ** len(stages)):
        return lax.psum(x, ("lon", "lat"))
    for axis, bit in stages:
        count = lax.axis_size(axis)
        side = (lax.axis_index(axis) // bit) % 2
        half = cur.shape[0] // 2
        keep = lax.dynamic_slice_in_dim(cur, side * half, half, 0)
        send = lax.dynamic_slice_in_dim(cur, (1 - side) * half, half, 0)
        sent = lax.ppermute(send.astype(jnp.bfloat16), axis, [(i, i ^ bit) for i in range(count)])
        cur = keep + sent.astype(cur.dtype)
    for axis, bit in reversed(stages):
        count = lax.axis_size(axis)
        side = (lax.axis_index(axis) // bit) % 2
        other = lax.ppermute(cur, axis, [(i, i ^ bit) for i in range(count)])
        half = cur.shape[0]
        buf = jnp.zeros((2 * half, cur.shape[1]), cur.dtype)
        buf = lax.dynamic_update_slice_in_dim(buf, cur, side * half, 0)
        cur = lax.dynamic_update_slice_in_dim(buf, other, (1 - side) * half, 0)
    return cur.reshape(x.shape)


def spread_block(source, coef_source, row_first, rows, col_first, cols):
    kernels = coef_source.shape[0]
    chans = source.shape[0]
    span = LON_REACH
    reach = LAT_REACH
    tap_count = 2 * span + 1
    window = cols + 2 * span
    tap_axis = jnp.arange(tap_count, dtype=jnp.int32)[:, None, None]
    wide_axis = jnp.arange(window, dtype=jnp.int32)[None, :, None]
    cell_axis = jnp.arange(cols, dtype=jnp.int32)[None, None, :]
    selector = (cell_axis + 2 * span - wide_axis == tap_axis).astype(jnp.bfloat16)
    total = jnp.zeros((kernels, chans, rows, cols), jnp.float32)
    for offset in range(2 * reach + 1):
        start = row_first + 2 * reach - offset
        rows_in = source[:, start : start + rows, col_first : col_first + window]
        part_coefs = coef_source[:, start : start + rows, offset, :]
        tiles = jnp.einsum(
            "bpq,kib->kipq", selector, part_coefs, preferred_element_type=jnp.float32
        ).astype(jnp.bfloat16)
        total = total + jnp.einsum(
            "oip,kipq->koiq", rows_in, tiles, preferred_element_type=jnp.float32
        )
    return total.astype(jnp.bfloat16)


def local(inputs, cotangent, mixing, filters, support):
    chans, lat_rows, lon_cols = inputs.shape
    span = LON_REACH
    reach = LAT_REACH
    tap_count = 2 * span + 1
    offsets = jnp.arange(tap_count, dtype=jnp.int32) - span
    keep = (jnp.abs(offsets)[None, :] <= support[:, None]).astype(jnp.bfloat16)
    coefs = filters * keep[None, :, None, :]
    widened = with_halo(cotangent, (("lon", 2),), span, True)
    padded = with_halo(widened, (("lat", 1),), reach, False)
    coef_pad = with_halo(coefs, (("lat", 1),), reach, False)
    spread = spread_block(padded, coef_pad, 0, lat_rows, 0, lon_cols)
    local_grad = jnp.einsum("koiq,ciq->koc", spread, inputs, preferred_element_type=jnp.float32)
    total_cells = lat_rows * lax.axis_size("lat") * lon_cols * lax.axis_size("lon")
    weight_grad = halving_psum(local_grad) * (1.0 / math.sqrt(total_cells))
    input_grad = jnp.einsum(
        "koc,koiq->ciq", mixing, spread, preferred_element_type=jnp.float32
    ).astype(jnp.bfloat16)
    return (input_grad, weight_grad)


def solution(mesh):
    return jax.shard_map(
        local,
        mesh=mesh,
        in_specs=(
            P(None, "lat", "lon"),
            P(None, "lat", "lon"),
            P(),
            P(None, "lat", None, None),
            P("lat"),
        ),
        out_specs=(P(None, "lat", "lon"), P()),
        check_vma=False,
    )
```

```python
import math

import jax
import jax.numpy as jnp
from jax import lax
from jax.sharding import PartitionSpec as P

LAT_REACH = 1
LON_REACH = 16


def with_halo(cells, sides, width, closed):
    for axis, dim in sides:
        count = lax.axis_size(axis)
        ends = count if closed else count - 1
        head = lax.slice_in_dim(cells, 0, width, axis=dim)
        tail = lax.slice_in_dim(cells, cells.shape[dim] - width, cells.shape[dim], axis=dim)
        cells = jnp.concatenate(
            [
                lax.ppermute(tail, axis, [(i, (i + 1) % count) for i in range(ends)]),
                cells,
                lax.ppermute(head, axis, [((i + 1) % count, i) for i in range(ends)]),
            ],
            axis=dim,
        )
    return cells


def halving_psum(x):
    stages = []
    for axis in ("lat", "lon"):
        bit = 1
        while bit < lax.axis_size(axis):
            stages.append((axis, bit))
            bit *= 2
    cur = x.reshape(-1, x.shape[-1])
    if cur.shape[0] % (2 ** len(stages)):
        return lax.psum(x, ("lon", "lat"))
    for axis, bit in stages:
        count = lax.axis_size(axis)
        side = (lax.axis_index(axis) // bit) % 2
        half = cur.shape[0] // 2
        keep = lax.dynamic_slice_in_dim(cur, side * half, half, 0)
        send = lax.dynamic_slice_in_dim(cur, (1 - side) * half, half, 0)
        sent = lax.ppermute(send.astype(jnp.bfloat16), axis, [(i, i ^ bit) for i in range(count)])
        cur = keep + sent.astype(cur.dtype)
    cur = cur.astype(jnp.bfloat16)
    for axis, bit in reversed(stages):
        count = lax.axis_size(axis)
        side = (lax.axis_index(axis) // bit) % 2
        other = lax.ppermute(cur, axis, [(i, i ^ bit) for i in range(count)])
        half = cur.shape[0]
        buf = jnp.zeros((2 * half, cur.shape[1]), cur.dtype)
        buf = lax.dynamic_update_slice_in_dim(buf, cur, side * half, 0)
        cur = lax.dynamic_update_slice_in_dim(buf, other, (1 - side) * half, 0)
    return cur.astype(x.dtype).reshape(x.shape)


def spread_block(source, coef_source, row_first, rows, col_first, cols):
    kernels = coef_source.shape[0]
    chans = source.shape[0]
    span = LON_REACH
    reach = LAT_REACH
    tap_count = 2 * span + 1
    window = cols + 2 * span
    tap_axis = jnp.arange(tap_count, dtype=jnp.int32)[:, None, None]
    wide_axis = jnp.arange(window, dtype=jnp.int32)[None, :, None]
    cell_axis = jnp.arange(cols, dtype=jnp.int32)[None, None, :]
    selector = (cell_axis + 2 * span - wide_axis == tap_axis).astype(jnp.bfloat16)
    total = jnp.zeros((kernels, chans, rows, cols), jnp.float32)
    for offset in range(2 * reach + 1):
        start = row_first + 2 * reach - offset
        rows_in = source[:, start : start + rows, col_first : col_first + window]
        part_coefs = coef_source[:, start : start + rows, offset, :]
        tiles = jnp.einsum(
            "bpq,kib->kipq", selector, part_coefs, preferred_element_type=jnp.float32
        ).astype(jnp.bfloat16)
        total = total + jnp.einsum(
            "oip,kipq->koiq", rows_in, tiles, preferred_element_type=jnp.float32
        )
    return total.astype(jnp.bfloat16)


def local(inputs, cotangent, mixing, filters, support):
    chans, lat_rows, lon_cols = inputs.shape
    span = LON_REACH
    reach = LAT_REACH
    tap_count = 2 * span + 1
    offsets = jnp.arange(tap_count, dtype=jnp.int32) - span
    keep = (jnp.abs(offsets)[None, :] <= support[:, None]).astype(jnp.bfloat16)
    coefs = filters * keep[None, :, None, :]
    widened = with_halo(cotangent, (("lon", 2),), span, True)
    padded = with_halo(widened, (("lat", 1),), reach, False)
    coef_pad = with_halo(coefs, (("lat", 1),), reach, False)
    spread = spread_block(padded, coef_pad, 0, lat_rows, 0, lon_cols)
    local_grad = jnp.einsum("koiq,ciq->koc", spread, inputs, preferred_element_type=jnp.float32)
    total_cells = lat_rows * lax.axis_size("lat") * lon_cols * lax.axis_size("lon")
    weight_grad = halving_psum(local_grad) * (1.0 / math.sqrt(total_cells))
    input_grad = jnp.einsum(
        "koc,koiq->ciq", mixing, spread, preferred_element_type=jnp.float32
    ).astype(jnp.bfloat16)
    return (input_grad, weight_grad)


def solution(mesh):
    return jax.shard_map(
        local,
        mesh=mesh,
        in_specs=(
            P(None, "lat", "lon"),
            P(None, "lat", "lon"),
            P(),
            P(None, "lat", None, None),
            P("lat"),
        ),
        out_specs=(P(None, "lat", "lon"), P()),
        check_vma=False,
    )
```
